128 devices in a mesh: wide: 32 (over y, x, core), narrow: 4 (over z).
Axes of the slice: x: 4, y: 4, z: 4, core: 2. Of those that a mesh axis runs over, the one named last changes fastest.
Arguments:
- amplitudes: float32 [4096, 8192], P(('wide', 'narrow')), may hold values from -6 to 6
- integrals: float32 [8192, 8192], P('narrow', 'wide'), may hold values from -0.1875 to 0.1875
- bare_terms: float32 [4096, 8192], P('wide', 'narrow'), may hold values from -6 to 6
- pattern: int32 [32, 64], replicated, may hold values 0 or 1
- block_order: int32 [32], replicated, may hold values from 0 to 31, each once
- occ_gap: float32 [4096], P('wide'), may hold values from 0.3 to 3
- virt_gap: float32 [8192], P('narrow'), may hold values from 0.3 to 3
Outputs:
- update: float32 [4096, 8192], P('wide', 'narrow')
The draws below stay inside these ranges and needn't reach their ends.
All inputs are finite; a program needn't handle non-finite values.
Results may differ from the reference program's by a relative error of at most 0.000054.
Values sent between devices are 32-bit elements; how exact they have to be, the bound alone decides.
A program may use at most 192 MiB of HBM per device.

```python
import math
import jax
import jax.numpy as jnp
from jax import lax

TILE = 128
VIR_TILES = 64
OCC_TILES = 32
PAIR_ROWS = 4096
VIRT_COLS = 8192


def plant(array, rng, low, largest):
    shape = array.shape
    place = [jax.random.randint(jax.random.fold_in(rng, axis), (), 0, shape[axis]) for axis in range(len(shape))]
    array = array.at[tuple(place)].set(low)
    longest = shape.index(max(shape))
    place[longest] = (place[longest] + 1) % shape[longest]
    return array.at[tuple(place)].set(largest)


def with_spikes(values, rng, source, target, shards_of, factor):
    def block_of(dim):
        return (jnp.arange(values.shape[dim]) // (values.shape[dim] // shards_of)).reshape((-1,) + (1,) * (values.ndim - 1 - dim))

    near = jax.random.permutation(rng, shards_of)[block_of(target)]
    far = (block_of(target) + shards_of // 2) % shards_of
    return jnp.where((block_of(source) == near) | (block_of(source) == far), factor * values, values)


def steps_of(own_key, extent, shards, least, high):
    def one(position, shards_of):
        steps = jax.random.uniform(jax.random.fold_in(jax.random.fold_in(own_key, 6), position), (shards_of,), jnp.float32, least / len(shards), high / len(shards))
        return jnp.repeat(jnp.exp(steps), extent[position] // shards_of).reshape((-1,) + (1,) * (len(extent) - position - 1))

    level = one(*shards[0])
    for cut in shards[1:]:
        level = level * one(*cut)
    return level


def noise(stream_key, dims, spread, reach, cuts=(), dtype=jnp.bfloat16):
    entries = spread * jax.random.normal(stream_key, dims, jnp.float32)
    if cuts:
        entries = entries * steps_of(stream_key, dims, cuts, -0.22, 0.18)
    return jnp.clip(entries, -reach, reach).astype(dtype)


def bell_draw_with(key, shape, spread, bound, shards, heavy, dtype=jnp.bfloat16):
    result = spread * jax.random.normal(key, shape, jnp.float32)
    if shards:
        result = result * steps_of(key, shape, shards, -0.22, 0.18)
    return jnp.clip(with_spikes(result, jax.random.fold_in(key, 3), *heavy), -bound, bound).astype(dtype)


def setup_inputs(seed: int = 0) -> dict:
    keys = jax.random.split(jax.random.key(seed), 8)
    return {
        "amplitudes": noise(keys[0], (PAIR_ROWS, VIRT_COLS), 1.0, 6.0, ((0, 128),), jnp.float32),
        "integrals": bell_draw_with(keys[1], (VIRT_COLS, VIRT_COLS), (VIRT_COLS // 2) ** -0.5, 0.1875, ((0, 4), (1, 32)), (0, 1, 32, 2.75), jnp.float32),
        "bare_terms": noise(keys[2], (PAIR_ROWS, VIRT_COLS), 1.0, 6.0, ((0, 32), (1, 4)), jnp.float32),
        "pattern": plant((jax.random.randint(keys[3], (OCC_TILES, VIR_TILES), 0, 2) < 1).astype(jnp.int32), jax.random.fold_in(keys[3], 1), 0, 1),
        "block_order": jax.random.permutation(keys[4], OCC_TILES).astype(jnp.int32),
        "occ_gap": jnp.clip(jnp.exp(math.log(3.0) - 2.3025851 * jax.random.uniform(keys[5], (PAIR_ROWS,), jnp.float32) ** steps_of(keys[5], (PAIR_ROWS,), ((0, 32),), -0.2, 0.2)), 0.3, 3.0),
        "virt_gap": jnp.clip(jnp.exp(math.log(3.0) - 2.3025851 * jax.random.uniform(keys[6], (VIRT_COLS,), jnp.float32) ** steps_of(keys[6], (VIRT_COLS,), ((0, 4),), -0.2, 0.2)), 0.3, 3.0),
    }


def reference(amplitudes, integrals, bare_terms, pattern, block_order, occ_gap, virt_gap):
    row_pattern = pattern[block_order.astype(jnp.int32)].astype(jnp.float32)
    full_mask = jnp.repeat(jnp.repeat(row_pattern, TILE, axis=0), TILE, axis=1)
    screened = amplitudes * full_mask
    ladder = jnp.dot(screened, integrals, preferred_element_type=jnp.float32, precision=lax.Precision.HIGHEST)
    return -(bare_terms + ladder) / (occ_gap[:, None] + virt_gap[None, :])
```

```python
import jax
import jax.numpy as jnp
from jax import lax
from jax.experimental import pallas as pl
from jax.experimental.pallas import tpu as pltpu
from jax.sharding import PartitionSpec as P

TILE = 128
MESH = pl.DeviceIdType.MESH
SEGMENTS = ((0, 256), (256, 256), (512, 256), (768, 128), (896, 128))
F32 = jnp.float32
BF16 = jnp.bfloat16


def kernel(
    amp, integ, bare_hbm, pattern, order, occ, virt, out,
    a_raw, a_hi, a_lo, b_own, b_left, b_right, b_far, b_hi, b_lo, part, other, total, final, bare, occ_wide,
    local_sem, b_send, b_recv, f_send, f_recv, az_send, az_recv, ay_send, ay_recv, af_send, af_recv,
    am_send, am_recv, rs_send, rs_recv, t_send, t_recv,
):
    w = lax.axis_index("wide")
    z = lax.axis_index("narrow")
    y = lax.div(w, 8)
    x = lax.rem(lax.div(w, 2), 4)
    c = lax.rem(w, 2)
    depth = integ.shape[0]
    half = depth // 2

    def device(yy, xx, cc, zz):
        return (yy * 8 + xx * 2 + cc, zz)

    def mod4(v):
        return lax.rem(v, 4)

    right, left = device(y, mod4(x + 1), c, z), device(y, mod4(x + 3), c, z)
    up, down = device(mod4(y + 1), x, c, z), device(mod4(y + 3), x, c, z)
    mate = device(y, x, 1 - c, z)
    deep = [None] + [device(y, x, c, mod4(z + d)) for d in (1, 2, 3)]
    swap = [device(z, x, c, y), device(z, x, 1 - c, y)]

    barrier = pltpu.get_barrier_semaphore()
    for who in (right, left, up, down, mate, deep[1], deep[2], deep[3]):
        pl.semaphore_signal(barrier, inc=1, device_id=who, device_id_type=MESH)

    @pl.when(y != z)
    def _():
        for who in swap:
            pl.semaphore_signal(barrier, inc=1, device_id=who, device_id_type=MESH)

    own_a = pltpu.make_async_copy(
        amp.at[:, pl.ds(pl.multiple_of(z * depth, depth), depth)],
        a_raw.at[0, 0, pl.ds(pl.multiple_of(z * 32, 32), 32)], local_sem.at[0])
    own_b = pltpu.make_async_copy(integ, b_own, local_sem.at[1])
    own_bare = pltpu.make_async_copy(bare_hbm, bare, local_sem.at[2])
    own_a.start()
    own_b.start()
    own_bare.start()

    @pl.when(y != z)
    def _():
        pl.semaphore_wait(barrier, 10)

    @pl.when(y == z)
    def _():
        pl.semaphore_wait(barrier, 8)

    def remote(src, dst, send, recv, who):
        return pltpu.make_async_remote_copy(
            src_ref=src, dst_ref=dst, send_sem=send, recv_sem=recv, device_id=who, device_id_type=MESH)

    def piece(q):
        return pl.ds(pl.multiple_of(q * 32, 32), 32)

    def columns(q):
        return pl.ds(pl.multiple_of(q * depth, depth), depth)

    def b_copy(h, d):
        return remote(
            integ.at[:, pl.ds(h * TILE, TILE)], (b_left, b_right)[d].at[:, pl.ds(h * TILE, TILE)],
            b_send.at[h, d], b_recv.at[h, d], (right, left)[d])

    def f_copy(h, d):
        rows = pl.ds(d * half, half)
        return remote(
            (b_left, b_right)[d].at[rows, pl.ds(h * TILE, TILE)], b_far.at[rows, pl.ds(h * TILE, TILE)],
            f_send.at[h, d], f_recv.at[h, d], (right, left)[d])

    def az_copy(d):
        return remote(
            amp.at[:, columns(mod4(z + d))], a_raw.at[0, 0, piece(z)], az_send.at[d], az_recv.at[z], deep[d])

    def az_arrived(q):
        return remote(
            amp.at[:, columns(q)], a_raw.at[0, 0, piece(q)], az_send.at[0], az_recv.at[q], mate)

    def ay_copy(q, d, first=False):
        src = amp.at[:, columns(z)] if first else a_raw.at[0, 0, piece(q)]
        return remote(
            src, a_raw.at[(3, 1)[d], 0, piece(q)], ay_send.at[d, q], ay_recv.at[d, q], (up, down)[d])

    def am_copy(q, first=False):
        src = amp.at[:, columns(z)] if first else a_raw.at[0, 0, piece(q)]
        return remote(src, a_raw.at[0, 1, piece(q)], am_send.at[q], am_recv.at[q], mate)

    def af_copy(q, d):
        dy = (3, 1)[d]
        return remote(
            a_raw.at[dy, 0, piece(q)], a_raw.at[2, 0, piece(q)], af_send.at[q], af_recv.at[q], (up, down)[d])

    def am_whole(dy):
        return remote(
            a_raw.at[dy, 0], a_raw.at[dy, 1], am_send.at[3 + dy], am_recv.at[3 + dy], mate)

    def rs_copy(s, dy):
        start, size = SEGMENTS[s]
        where = pl.ds(start, size)
        target = mod4(y + dy)
        return remote(
            part.at[dy, :, where], other.at[z, :, where], rs_send.at[s, dy], rs_recv.at[s, z],
            device(y, x, c, target))

    def rs_arrived(s, q):
        start, size = SEGMENTS[s]
        where = pl.ds(start, size)
        return remote(
            part.at[0, :, where], other.at[q, :, where], rs_send.at[s, 0], rs_recv.at[s, q], mate)

    def t_copy(s, r):
        start, size = SEGMENTS[s]
        where = pl.ds(start, size)
        return remote(
            total.at[pl.ds(r * TILE, TILE), where], final.at[r, :, where], t_send.at[s, r], t_recv.at[s, r], swap[r])

    def t_local(s):
        start, size = SEGMENTS[s]
        where = pl.ds(start, size)
        return pltpu.make_async_copy(total.at[pl.ds(0, TILE), where], final.at[0, :, where], t_recv.at[s, 0])

    for h in range(2):
        for d in range(2):
            b_copy(h, d).start()
    for d in (1, 3, 2):
        az_copy(d).start()
    for d in range(2):
        ay_copy(z, d, True).start()
    am_copy(z, True).start()

    def split(value):
        hi = value.astype(BF16)
        return hi, (value - hi.astype(F32)).astype(BF16)

    def convert_b(slot, sources):
        @pl.loop(0, depth // 256)
        def _(i):
            rows = pl.ds(pl.multiple_of(i * 256, 256), 256)
            for at, source, start in sources:
                hi, lo = split(source[rows, start:start + TILE])
                b_hi[slot, rows, at:at + TILE] = hi
                b_lo[slot, rows, at:at + TILE] = lo

    def convert_a(dy, rel):
        tile = mod4(y + dy) * 8 + x * 2 + lax.rem(c + rel, 2)
        block = order[tile]

        @pl.loop(0, depth // TILE)
        def _(k):
            keep = pattern[block, z * (depth // TILE) + k].astype(F32)
            where = pl.ds(pl.multiple_of(k * TILE, TILE), TILE)
            hi, lo = split(a_raw[dy, rel, :, where] * keep)
            a_hi[dy, rel * TILE:(rel + 1) * TILE, where] = hi
            a_lo[dy, rel * TILE:(rel + 1) * TILE, where] = lo

    def dot(a, b):
        return jnp.dot(a, b, preferred_element_type=F32)

    def multiply(s, dy):
        start, size = SEGMENTS[s]
        slot, at = start // 256, start % 256
        hi, lo = b_hi[slot, :, at:at + size], b_lo[slot, :, at:at + size]
        left_hi, left_lo = a_hi[dy], a_lo[dy]
        part[dy, :, start:start + size] = dot(left_hi, hi) + (dot(left_hi, lo) + dot(left_lo, hi))

        @pl.when(mod4(y + dy) != z)
        def _():
            rs_copy(s, dy).start()

    def add_up(s):
        start, size = SEGMENTS[s]
        for d in (1, 3, 2):
            rs_arrived(s, mod4(z + d)).wait_recv()
        mine = mod4(z + 4 - y)

        @pl.loop(0, 4)
        def _(i):
            rows = pl.ds(pl.multiple_of(i * 64, 64), 64)
            value = part[mine, rows, start:start + size]
            for d in (1, 2, 3):
                value = value + other[mod4(z + d), rows, start:start + size]
            total[rows, start:start + size] = value

        t_copy(s, 1).start()

        @pl.when(y != z)
        def _():
            t_copy(s, 0).start()

        @pl.when(y == z)
        def _():
            t_local(s).start()

    def finish(s):
        start, size = SEGMENTS[s]

        @pl.when(y != z)
        def _():
            t_copy(s, 0).wait_recv()

        @pl.when(y == z)
        def _():
            t_local(s).wait()

        t_copy(s, 1).wait_recv()
        beside = mod4(x + 3), mod4(x + 1)
        pieces = (
            ((x, 0), (x, 1)), ((beside[0], 0), (beside[1], 0)), ((beside[0], 1), (beside[1], 1)),
            ((mod4(x + 2), 0),), ((mod4(x + 2), 1),))[s]
        for r in range(2):
            for i, (xx, h) in enumerate(pieces):
                place = pl.multiple_of(xx * 512 + lax.rem(c + r, 2) * 256 + h * TILE, TILE)
                where = pl.ds(place, TILE)
                value = bare[:, where] + final[r, :, start + i * TILE:start + (i + 1) * TILE]
                out[:, where] = -value / (occ_wide[...] + virt[:, where])

    own_b.wait()
    convert_b(0, ((0, b_own, 0), (TILE, b_own, TILE)))
    occ_wide[...] = jnp.broadcast_to(occ[...], (TILE, TILE)).T
    own_a.wait()

    for d in (1, 3, 2):
        q = mod4(z + d)
        az_arrived(q).wait_recv()
        for to in range(2):
            ay_copy(q, to).start()
        am_copy(q).start()
    convert_a(0, 0)
    for d in (0, 1, 3, 2):
        am_copy(mod4(z + d)).wait_recv()
    convert_a(0, 1)
    multiply(0, 0)

    for q, d in ((z, 0), (mod4(z + 1), 0), (mod4(z + 3), 1), (mod4(z + 2), 1)):
        ay_copy(q, d).wait_recv()
        af_copy(q, d).start()
    for q, d in ((z, 1), (mod4(z + 1), 1), (mod4(z + 3), 0), (mod4(z + 2), 0)):
        ay_copy(q, d).wait_recv()
    am_whole(3).start()
    am_whole(1).start()
    for d in range(2):
        b_copy(0, d).wait_recv()
        f_copy(0, d).start()
    convert_a(3, 0)
    convert_a(1, 0)
    am_whole(3).wait_recv()
    convert_a(3, 1)
    am_whole(1).wait_recv()
    convert_a(1, 1)
    multiply(0, 3)
    multiply(0, 1)
    convert_b(1, ((0, b_left, 0), (TILE, b_right, 0)))
    for dy in (0, 3, 1):
        multiply(1, dy)

    for d in range(4):
        af_copy(mod4(z + d), 0).wait_recv()
    am_whole(2).start()
    convert_a(2, 0)
    am_whole(2).wait_recv()
    convert_a(2, 1)
    multiply(0, 2)
    multiply(1, 2)

    for d in range(2):
        b_copy(1, d).wait_recv()
        f_copy(1, d).start()
    convert_b(2, ((0, b_left, TILE), (TILE, b_right, TILE)))

    @pl.loop(0, 4)
    def _(dy):
        multiply(2, dy)

    add_up(0)
    add_up(1)
    own_bare.wait()

    for d in range(2):
        f_copy(0, d).wait_recv()
    convert_b(3, ((0, b_far, 0),))

    @pl.loop(0, 4)
    def _(dy):
        multiply(3, dy)

    finish(0)
    finish(1)
    add_up(2)

    for d in range(2):
        f_copy(1, d).wait_recv()
    convert_b(3, ((TILE, b_far, TILE),))

    @pl.loop(0, 4)
    def _(dy):
        multiply(4, dy)

    add_up(3)
    finish(2)
    add_up(4)
    finish(3)
    finish(4)

    for h in range(2):
        for d in range(2):
            b_copy(h, d).wait_send()
            f_copy(h, d).wait_send()
    for d in (1, 2, 3):
        az_copy(d).wait_send()
        am_whole(d).wait_send()
    for d in range(4):
        q = mod4(z + d)
        for to in range(2):
            ay_copy(q, to).wait_send()
        am_copy(q).wait_send()
        af_copy(q, 0).wait_send()
    for s in range(len(SEGMENTS)):
        for dy in range(4):
            @pl.when(mod4(y + dy) != z)
            def _():
                rs_copy(s, dy).wait_send()

        t_copy(s, 1).wait_send()

        @pl.when(y != z)
        def _():
            t_copy(s, 0).wait_send()


def shards(amplitudes, integrals, bare_terms, pattern, block_order, occ_gap, virt_gap):
    depth, width = integrals.shape
    rows, columns = bare_terms.shape
    anywhere = pl.BlockSpec(memory_space=pl.ANY)
    vector = pl.BlockSpec(memory_space=pltpu.VMEM)
    scalar = pl.BlockSpec(memory_space=pltpu.SMEM)
    sems = [(3,), (2, 2), (2, 2), (2, 2), (2, 2), (4,), (4,), (2, 4), (2, 4), (4,), (4,), (7,), (7,),
            (5, 4), (5, 4), (5, 2), (5, 2)]
    return pl.pallas_call(
        kernel,
        out_shape=jax.ShapeDtypeStruct((rows, columns), F32),
        in_specs=[anywhere, anywhere, anywhere, scalar, scalar, vector, vector],
        out_specs=vector,
        scratch_shapes=[
            pltpu.VMEM((4, 2, TILE, depth), F32),
            pltpu.VMEM((4, 2 * TILE, depth), BF16),
            pltpu.VMEM((4, 2 * TILE, depth), BF16),
            pltpu.VMEM((depth, width), F32),
            pltpu.VMEM((depth, width), F32),
            pltpu.VMEM((depth, width), F32),
            pltpu.VMEM((depth, width), F32),
            pltpu.VMEM((4, depth, width), BF16),
            pltpu.VMEM((4, depth, width), BF16),
            pltpu.VMEM((4, 2 * TILE, 4 * width), F32),
            pltpu.VMEM((4, 2 * TILE, 4 * width), F32),
            pltpu.VMEM((2 * TILE, 4 * width), F32),
            pltpu.VMEM((2, TILE, 4 * width), F32),
            pltpu.VMEM((rows, columns), F32),
            pltpu.VMEM((TILE, TILE), F32),
        ] + [pltpu.SemaphoreType.DMA(shape) for shape in sems],
        compiler_params=pltpu.CompilerParams(
            collective_id=0, has_side_effects=True, vmem_limit_bytes=58 * 2**20),
        name="ladder",
    )(amplitudes, integrals, bare_terms, pattern, block_order, occ_gap.reshape(1, -1), virt_gap.reshape(1, -1))


def solution(mesh):
    placed = (
        P(("wide", "narrow"), None),
        P("narrow", "wide"),
        P("wide", "narrow"),
        P(),
        P(),
        P("wide"),
        P("narrow"),
    )
    return jax.shard_map(
        shards, mesh=mesh, in_specs=placed, out_specs=P("wide", "narrow"), check_vma=False
    )
```

```python
import jax
import jax.numpy as jnp
from jax import lax
from jax.experimental import pallas as pl
from jax.experimental.pallas import tpu as pltpu
from jax.sharding import PartitionSpec as P

TILE = 128
MESH = pl.DeviceIdType.MESH
SEGMENTS = ((0, 256), (256, 256), (512, 256), (768, 128), (896, 128))
DIRECT = (4,)
DIRECT_START = 768
F32 = jnp.float32
BF16 = jnp.bfloat16


def kernel(
    amp, integ, bare_hbm, pattern, order, occ, virt, out,
    a_raw, a_hi, a_lo, b_own, b_left, b_right, b_far, b_hi, b_lo, part, passing, other, total, hop, final, middle, gathered, bare, occ_wide,
    local_sem, b_send, b_recv, f_send, f_recv, az_send, az_recv, ay_send, ay_recv, af_send, af_recv,
    am_send, am_recv, p_send, p_recv, n_send, n_recv, t_send, t_recv, h_send, h_recv,
    d_send, d_recv, m_send, m_recv,
):
    w = lax.axis_index("wide")
    z = lax.axis_index("narrow")
    y = lax.div(w, 8)
    x = lax.rem(lax.div(w, 2), 4)
    c = lax.rem(w, 2)
    depth = integ.shape[0]
    half = depth // 2

    def device(yy, xx, cc, zz):
        return (yy * 8 + xx * 2 + cc, zz)

    def mod4(v):
        return lax.rem(v, 4)

    right, left = device(y, mod4(x + 1), c, z), device(y, mod4(x + 3), c, z)
    up, down = device(mod4(y + 1), x, c, z), device(mod4(y + 3), x, c, z)
    mate = device(y, x, 1 - c, z)
    deep = [None] + [device(y, x, c, mod4(z + d)) for d in (1, 2, 3)]
    barrier = pltpu.get_barrier_semaphore()
    greeted = [right, left, mate]
    for d in (1, 2, 3):
        for cc in (c, 1 - c):
            greeted += [device(mod4(y + d), x, cc, z), device(y, x, cc, mod4(z + d))]
    for who in greeted:
        pl.semaphore_signal(barrier, inc=1, device_id=who, device_id_type=MESH)

    own_a = pltpu.make_async_copy(
        amp.at[:, pl.ds(pl.multiple_of(z * depth, depth), depth)],
        a_raw.at[0, 0, pl.ds(pl.multiple_of(z * 32, 32), 32)], local_sem.at[0])
    own_b = pltpu.make_async_copy(integ, b_own, local_sem.at[1])
    own_bare = pltpu.make_async_copy(bare_hbm, bare, local_sem.at[2])
    own_a.start()
    own_b.start()
    own_bare.start()

    pl.semaphore_wait(barrier, len(greeted))

    def remote(src, dst, send, recv, who):
        return pltpu.make_async_remote_copy(
            src_ref=src, dst_ref=dst, send_sem=send, recv_sem=recv, device_id=who, device_id_type=MESH)

    def piece(q):
        return pl.ds(pl.multiple_of(q * 32, 32), 32)

    def columns(q):
        return pl.ds(pl.multiple_of(q * depth, depth), depth)

    def b_copy(h, d):
        return remote(
            integ.at[:, pl.ds(h * TILE, TILE)], (b_left, b_right)[d].at[:, pl.ds(h * TILE, TILE)],
            b_send.at[h, d], b_recv.at[h, d], (right, left)[d])

    def f_copy(h, d):
        rows = pl.ds(d * half, half)
        return remote(
            (b_left, b_right)[d].at[rows, pl.ds(h * TILE, TILE)], b_far.at[rows, pl.ds(h * TILE, TILE)],
            f_send.at[h, d], f_recv.at[h, d], (right, left)[d])

    def az_copy(d):
        return remote(
            amp.at[:, columns(mod4(z + d))], a_raw.at[0, 0, piece(z)], az_send.at[d], az_recv.at[z], deep[d])

    def az_arrived(q):
        return remote(
            amp.at[:, columns(q)], a_raw.at[0, 0, piece(q)], az_send.at[0], az_recv.at[q], mate)

    def ay_copy(q, d, first=False):
        src = amp.at[:, columns(z)] if first else a_raw.at[0, 0, piece(q)]
        return remote(
            src, a_raw.at[(3, 1)[d], 0, piece(q)], ay_send.at[d, q], ay_recv.at[d, q], (up, down)[d])

    def am_copy(q, first=False):
        src = amp.at[:, columns(z)] if first else a_raw.at[0, 0, piece(q)]
        return remote(src, a_raw.at[0, 1, piece(q)], am_send.at[q], am_recv.at[q], mate)

    def af_copy(q, d):
        dy = (3, 1)[d]
        return remote(
            a_raw.at[dy, 0, piece(q)], a_raw.at[2, 0, piece(q)], af_send.at[q], af_recv.at[q], (up, down)[d])

    def am_far(q):
        return remote(
            a_raw.at[2, 0, piece(q)], a_raw.at[2, 1, piece(q)], am_send.at[8 + q], am_recv.at[8 + q], mate)

    def am_whole(dy):
        return remote(
            a_raw.at[dy, 0], a_raw.at[dy, 1], am_send.at[3 + dy], am_recv.at[3 + dy], mate)

    def area(s, r):
        start, size = SEGMENTS[s]
        return pl.ds(r * TILE, TILE), pl.ds(start, size)

    def p_copy(s, dy, d):
        rows, where = area(s, d)
        return remote(
            part.at[dy, rows, where], passing.at[d, :, where], p_send.at[s, d], p_recv.at[s, d], (deep[1], deep[3])[d])

    def n_copy(s, dy, d, r):
        rows, where = area(s, r)
        return remote(
            part.at[dy, rows, where], other.at[d, rows, where], n_send.at[s, d, r], n_recv.at[s, d, r],
            (deep[1], deep[3])[d])

    def row_of(s):
        return mod4(z + 8 - y - s)

    column_of = row_of

    def t_copy(s, r, last):
        rows, where = area(s, r)
        return remote(
            total.at[rows, where], (final if last else hop).at[r, :, where], t_send.at[s, r],
            (t_recv if last else h_recv).at[s, r], device(row_of(s), x, lax.rem(c + r, 2), z))

    def h_copy(s, r, straight=False):
        rows, where = area(s, r)
        return remote(
            total.at[rows, where] if straight else hop.at[r, :, where], final.at[r, :, where], h_send.at[s, r],
            t_recv.at[s, r], device(y, x, c, column_of(s)))

    def t_local(s):
        rows, where = area(s, 0)
        return pltpu.make_async_copy(total.at[rows, where], final.at[0, :, where], t_recv.at[s, 0])

    def relay(s):
        @pl.when(mod4(y + s) != 0)
        def _():
            t_copy(s, 1, False).wait_recv()
            h_copy(s, 1).start()

            @pl.when(column_of(s) != y)
            def _():
                t_copy(s, 0, False).wait_recv()
                h_copy(s, 0).start()

    def spot(s, r):
        start, size = SEGMENTS[s]
        return pl.ds(r * TILE, TILE), pl.ds(start, size), pl.ds(start - DIRECT_START, size)

    def y_copy(s, dy, r, final_stop):
        rows, where, there = spot(s, r)
        return remote(
            part.at[dy, rows, where],
            gathered.at[z, rows, there] if final_stop else middle.at[dy, rows, there],
            d_send.at[s, dy, r], d_recv.at[s, z, r] if final_stop else m_recv.at[s, dy, r],
            device(mod4(y + dy), x, lax.rem(c + r, 2), z))

    def z_copy(s, r):
        rows, where, there = spot(s, r)
        return remote(
            part.at[0, rows, where], gathered.at[z, rows, there], d_send.at[s, 0, r], d_recv.at[s, z, r],
            device(y, x, lax.rem(c + r, 2), y))

    def pass_on_product(s, dy, r):
        rows, where, there = spot(s, r)
        return remote(
            middle.at[dy, rows, there], gathered.at[z, rows, there], m_send.at[s, dy, r], d_recv.at[s, z, r],
            device(y, x, c, mod4(y + 4 - dy)))

    def m_arrived(s, dy, r):
        rows, where, there = spot(s, r)
        return remote(
            part.at[0, rows, where], middle.at[dy, rows, there], m_send.at[s, dy, r], m_recv.at[s, dy, r], mate)

    def d_local(s):
        rows, where, there = spot(s, 0)
        return pltpu.make_async_copy(part.at[0, rows, where], gathered.at[z, rows, there], d_recv.at[s, z, 0])

    def d_arrived(s, q, r):
        rows, where, there = spot(s, r)
        return remote(
            part.at[0, rows, where], gathered.at[q, rows, there], d_send.at[s, 0, r], d_recv.at[s, q, r], mate)

    def forward(s):
        for dy in (1, 3, 2):
            @pl.when(mod4(y + 4 - dy) != z)
            def _():
                for r in range(2):
                    m_arrived(s, dy, r).wait_recv()
                    pass_on_product(s, dy, r).start()

    def block_for(s, delta):
        return mod4(z + delta + 16 - 2 * y - s)

    for h in range(2):
        for d in range(2):
            b_copy(h, d).start()
    for d in (1, 3, 2):
        az_copy(d).start()
    for d in range(2):
        ay_copy(z, d, True).start()
    am_copy(z, True).start()

    def split(value):
        hi = value.astype(BF16)
        return hi, (value - hi.astype(F32)).astype(BF16)

    def convert_b(slot, sources):
        @pl.loop(0, depth // 256)
        def _(i):
            rows = pl.ds(pl.multiple_of(i * 256, 256), 256)
            for at, source, start in sources:
                hi, lo = split(source[rows, start:start + TILE])
                b_hi[slot, rows, at:at + TILE] = hi
                b_lo[slot, rows, at:at + TILE] = lo

    def convert_a(dy, rel):
        tile = mod4(y + dy) * 8 + x * 2 + lax.rem(c + rel, 2)
        block = order[tile]

        @pl.loop(0, depth // TILE)
        def _(k):
            keep = pattern[block, z * (depth // TILE) + k].astype(F32)
            where = pl.ds(pl.multiple_of(k * TILE, TILE), TILE)
            hi, lo = split(a_raw[dy, rel, :, where] * keep)
            a_hi[dy, rel * TILE:(rel + 1) * TILE, where] = hi
            a_lo[dy, rel * TILE:(rel + 1) * TILE, where] = lo

    def dot(a, b):
        return jnp.dot(a, b, preferred_element_type=F32)

    def multiply(s, dy):
        start, size = SEGMENTS[s]
        slot, at = start // 256, start % 256
        hi, lo = b_hi[slot, :, at:at + size], b_lo[slot, :, at:at + size]
        left_hi, left_lo = a_hi[dy], a_lo[dy]
        part[dy, :, start:start + size] = dot(left_hi, hi) + (dot(left_hi, lo) + dot(left_lo, hi))

        if s in DIRECT:
            @pl.when(dy == 0)
            def _():
                z_copy(s, 1).start()

                @pl.when(y != z)
                def _():
                    z_copy(s, 0).start()

                @pl.when(y == z)
                def _():
                    d_local(s).start()

            @pl.when(jnp.logical_and(dy != 0, y != z))
            def _():
                for r in range(2):
                    y_copy(s, dy, r, False).start()

            @pl.when(jnp.logical_and(dy != 0, y == z))
            def _():
                for r in range(2):
                    y_copy(s, dy, r, True).start()
        else:
            delta = mod4(2 * y + dy + s + 4 - z)

            @pl.when(delta == 2)
            def _():
                for d in range(2):
                    p_copy(s, dy, d).start()

            @pl.when(delta == 1)
            def _():
                n_copy(s, dy, 0, 1).start()

            @pl.when(delta == 3)
            def _():
                n_copy(s, dy, 1, 0).start()

    def pass_on(s, dy):
        if s in DIRECT:
            return
        start, size = SEGMENTS[s]
        delta = mod4(2 * y + dy + s + 4 - z)
        for d in range(2):
            @pl.when(delta == (1, 3)[d])
            def _():
                p_copy(s, 0, d).wait_recv()
                rows = slice(d * TILE, (d + 1) * TILE)
                part[dy, rows, start:start + size] += passing[d, :, start:start + size]
                n_copy(s, dy, d, d).start()

    def add_up(s):
        start, size = SEGMENTS[s]
        mine = block_for(s, 0)
        for r in (1, 0):
            for d in range(2):
                n_copy(s, 0, d, r).wait_recv()
            rows = slice(r * TILE, (r + 1) * TILE)
            where = slice(start, start + size)
            total[rows, where] = part[mine, rows, where] + (other[0, rows, where] + other[1, rows, where])
            send_total(s, r)

    def send_total(s, r):
        def go(last):
            if r == 1:
                t_copy(s, r, last).start()
            else:
                @pl.when(row_of(s) != y)
                def _():
                    t_copy(s, r, last).start()

                @pl.when(row_of(s) == y)
                def _():
                    if last:
                        t_local(s).start()
                    else:
                        h_copy(s, 0, True).start()

        @pl.when(mod4(row_of(s) + s) == 0)
        def _():
            go(True)

        @pl.when(mod4(row_of(s) + s) != 0)
        def _():
            go(False)

    def finish(s):
        start, size = SEGMENTS[s]
        if s in DIRECT:
            for q in range(4):
                d_arrived(s, q, 1).wait_recv()

                @pl.when(jnp.logical_or(y != z, q != z))
                def _():
                    d_arrived(s, q, 0).wait_recv()

            @pl.when(y == z)
            def _():
                d_local(s).wait()
        else:
            here = jnp.logical_and(mod4(y + s) == 0, y == z)

            @pl.when(jnp.logical_not(here))
            def _():
                h_copy(s, 0).wait_recv()

            @pl.when(here)
            def _():
                t_local(s).wait()

            h_copy(s, 1).wait_recv()
        beside = mod4(x + 3), mod4(x + 1)
        pieces = (
            ((x, 0), (x, 1)), ((beside[0], 0), (beside[1], 0)), ((beside[0], 1), (beside[1], 1)),
            ((mod4(x + 2), 0),), ((mod4(x + 2), 1),))[s]
        for r in range(2):
            for i, (xx, h) in enumerate(pieces):
                place = pl.multiple_of(xx * 512 + lax.rem(c + r, 2) * 256 + h * TILE, TILE)
                where = pl.ds(place, TILE)
                at = start + i * TILE
                if s in DIRECT:
                    at = at - DIRECT_START
                    mine = [gathered[q, r * TILE:(r + 1) * TILE, at:at + TILE] for q in range(4)]
                    value = bare[:, where] + ((mine[0] + mine[1]) + (mine[2] + mine[3]))
                else:
                    value = bare[:, where] + final[r, :, at:at + TILE]
                out[:, where] = -value / (occ_wide[...] + virt[:, where])

    own_b.wait()
    convert_b(0, ((0, b_own, 0), (TILE, b_own, TILE)))
    occ_wide[...] = jnp.broadcast_to(occ[...], (TILE, TILE)).T
    own_a.wait()

    for d in (1, 3, 2):
        q = mod4(z + d)
        az_arrived(q).wait_recv()
        for to in range(2):
            ay_copy(q, to).start()
        am_copy(q).start()
    convert_a(0, 0)
    for d in (0, 1, 3, 2):
        am_copy(mod4(z + d)).wait_recv()
    convert_a(0, 1)
    multiply(0, jnp.int32(0))

    for q, d in ((z, 0), (mod4(z + 1), 0), (mod4(z + 3), 1), (mod4(z + 2), 1)):
        ay_copy(q, d).wait_recv()
        af_copy(q, d).start()
    for q, d in ((z, 1), (mod4(z + 1), 1), (mod4(z + 3), 0), (mod4(z + 2), 0)):
        ay_copy(q, d).wait_recv()
    am_whole(3).start()
    am_whole(1).start()
    for d in range(2):
        b_copy(0, d).wait_recv()
        f_copy(0, d).start()
    convert_a(3, 0)
    convert_a(1, 0)
    am_whole(3).wait_recv()
    convert_a(3, 1)
    am_whole(1).wait_recv()
    convert_a(1, 1)
    multiply(0, jnp.int32(3))
    multiply(0, jnp.int32(1))
    pass_on(0, 0)
    convert_b(1, ((0, b_left, 0), (TILE, b_right, 0)))
    for dy in (0, 3, 1):
        multiply(1, jnp.int32(dy))
    for q, d in ((z, 0), (mod4(z + 1), 0), (mod4(z + 3), 1), (mod4(z + 2), 1)):
        af_copy(q, d).wait_recv()
        am_far(q).start()
    pass_on(0, 3)
    pass_on(0, 1)
    convert_a(2, 0)
    for d in (0, 1, 3, 2):
        am_far(mod4(z + d)).wait_recv()
    convert_a(2, 1)
    multiply(0, jnp.int32(2))
    multiply(1, jnp.int32(2))
    pass_on(1, 0)
    pass_on(1, 3)
    pass_on(1, 1)

    for d in range(2):
        b_copy(1, d).wait_recv()
        f_copy(1, d).start()
    pass_on(0, 2)
    convert_b(2, ((0, b_left, TILE), (TILE, b_right, TILE)))
    pass_on(1, 2)

    def every(order, action, s):
        @pl.loop(0, 4)
        def _(i):
            action(s, mod4(3 * i + order))

    every(0, multiply, 2)
    every(0, pass_on, 2)
    add_up(0)
    add_up(1)
    own_bare.wait()

    for d in range(2):
        f_copy(0, d).wait_recv()
    convert_b(3, ((0, b_far, 0),))
    every(1, multiply, 3)
    every(1, pass_on, 3)
    add_up(2)

    for d in range(2):
        f_copy(1, d).wait_recv()
    convert_b(3, ((TILE, b_far, TILE),))
    every(1, multiply, 4)
    add_up(3)
    relay(0)
    relay(1)
    relay(2)
    forward(4)
    relay(3)
    for s in range(5):
        finish(s)

    for h in range(2):
        for d in range(2):
            b_copy(h, d).wait_send()
            f_copy(h, d).wait_send()
    for d in (1, 2, 3):
        az_copy(d).wait_send()
    for d in (1, 3):
        am_whole(d).wait_send()
    for d in range(4):
        q = mod4(z + d)
        for to in range(2):
            ay_copy(q, to).wait_send()
        am_copy(q).wait_send()
        af_copy(q, 0).wait_send()
        am_far(q).wait_send()
    for s in range(len(SEGMENTS)):
        if s in DIRECT:
            @pl.when(y != z)
            def _():
                z_copy(s, 0).wait_send()

            z_copy(s, 1).wait_send()

            @pl.loop(1, 4)
            def _(dy):
                for r in range(2):
                    y_copy(s, dy, r, False).wait_send()

                @pl.when(mod4(y + 4 - dy) != z)
                def _():
                    for r in range(2):
                        pass_on_product(s, dy, r).wait_send()
        else:
            for d in range(2):
                p_copy(s, 0, d).wait_send()
                for r in range(2):
                    n_copy(s, 0, d, r).wait_send()
            t_copy(s, 1, True).wait_send()

            @pl.when(row_of(s) != y)
            def _():
                t_copy(s, 0, True).wait_send()

            @pl.when(mod4(y + s) != 0)
            def _():
                for r in range(2):
                    h_copy(s, r).wait_send()


def shards(amplitudes, integrals, bare_terms, pattern, block_order, occ_gap, virt_gap):
    depth, width = integrals.shape
    rows, columns = bare_terms.shape
    anywhere = pl.BlockSpec(memory_space=pl.ANY)
    vector = pl.BlockSpec(memory_space=pltpu.VMEM)
    scalar = pl.BlockSpec(memory_space=pltpu.SMEM)
    sems = [(3,), (2, 2), (2, 2), (2, 2), (2, 2), (4,), (4,), (2, 4), (2, 4), (4,), (4,), (12,), (12,),
            (5, 2), (5, 2), (5, 2, 2), (5, 2, 2), (5, 2), (5, 2), (5, 2), (5, 2),
            (5, 4, 2), (5, 4, 2), (5, 4, 2), (5, 4, 2)]
    return pl.pallas_call(
        kernel,
        out_shape=jax.ShapeDtypeStruct((rows, columns), F32),
        in_specs=[anywhere, anywhere, anywhere, scalar, scalar, vector, vector],
        out_specs=vector,
        scratch_shapes=[
            pltpu.VMEM((4, 2, TILE, depth), F32),
            pltpu.VMEM((4, 2 * TILE, depth), BF16),
            pltpu.VMEM((4, 2 * TILE, depth), BF16),
            pltpu.VMEM((depth, width), F32),
            pltpu.VMEM((depth, width), F32),
            pltpu.VMEM((depth, width), F32),
            pltpu.VMEM((depth, width), F32),
            pltpu.VMEM((4, depth, width), BF16),
            pltpu.VMEM((4, depth, width), BF16),
            pltpu.VMEM((4, 2 * TILE, 4 * width), F32),
            pltpu.VMEM((2, TILE, 4 * width), F32),
            pltpu.VMEM((2, 2 * TILE, 4 * width), F32),
            pltpu.VMEM((2 * TILE, 4 * width), F32),
            pltpu.VMEM((2, TILE, 4 * width), F32),
            pltpu.VMEM((2, TILE, 4 * width), F32),
            pltpu.VMEM((4, 2 * TILE, width), F32),
            pltpu.VMEM((4, 2 * TILE, width), F32),
            pltpu.VMEM((rows, columns), F32),
            pltpu.VMEM((TILE, TILE), F32),
        ] + [pltpu.SemaphoreType.DMA(shape) for shape in sems],
        compiler_params=pltpu.CompilerParams(
            collective_id=0, has_side_effects=True, vmem_limit_bytes=58 * 2**20),
        name="ladder",
    )(amplitudes, integrals, bare_terms, pattern, block_order, occ_gap.reshape(1, -1), virt_gap.reshape(1, -1))


def solution(mesh):
    placed = (
        P(("wide", "narrow"), None),
        P("narrow", "wide"),
        P("wide", "narrow"),
        P(),
        P(),
        P("wide"),
        P("narrow"),
    )
    return jax.shard_map(
        shards, mesh=mesh, in_specs=placed, out_specs=P("wide", "narrow"), check_vma=False
    )
```

```python
import jax
import jax.numpy as jnp
from jax import lax
from jax.experimental import pallas as pl
from jax.experimental.pallas import tpu as pltpu
from jax.sharding import PartitionSpec as P

TILE = 128
MESH = pl.DeviceIdType.MESH
SEGMENTS = ((0, 256), (256, 256), (512, 256), (768, 128), (896, 128))
DIRECT = (4,)
DIRECT_START = 768
F32 = jnp.float32
BF16 = jnp.bfloat16


def kernel(
    amp, integ, bare_hbm, pattern, order, occ, virt, out,
    a_raw, a_hi, a_lo, b_own, b_left, b_right, b_far, b_hi, b_lo, part, passing, other, total, hop, final, middle, gathered, bare, occ_wide,
    local_sem, b_send, b_recv, f_send, f_recv, az_send, az_recv, ay_send, ay_recv, af_send, af_recv,
    am_send, am_recv, p_send, p_recv, n_send, n_recv, t_send, t_recv, h_send, h_recv,
    d_send, d_recv, m_send, m_recv,
):
    w = lax.axis_index("wide")
    z = lax.axis_index("narrow")
    y = lax.div(w, 8)
    x = lax.rem(lax.div(w, 2), 4)
    c = lax.rem(w, 2)
    depth = integ.shape[0]
    half = depth // 2

    def device(yy, xx, cc, zz):
        return (yy * 8 + xx * 2 + cc, zz)

    def mod4(v):
        return lax.rem(v, 4)

    right, left = device(y, mod4(x + 1), c, z), device(y, mod4(x + 3), c, z)
    up, down = device(mod4(y + 1), x, c, z), device(mod4(y + 3), x, c, z)
    mate = device(y, x, 1 - c, z)
    deep = [None] + [device(y, x, c, mod4(z + d)) for d in (1, 2, 3)]
    barrier = pltpu.get_barrier_semaphore()
    greeted = [right, left, mate]
    for d in (1, 2, 3):
        for cc in (c, 1 - c):
            greeted += [device(mod4(y + d), x, cc, z), device(y, x, cc, mod4(z + d))]
    for who in greeted:
        pl.semaphore_signal(barrier, inc=1, device_id=who, device_id_type=MESH)

    own_a = pltpu.make_async_copy(
        amp.at[:, pl.ds(pl.multiple_of(z * depth, depth), depth)],
        a_raw.at[0, 0, pl.ds(pl.multiple_of(z * 32, 32), 32)], local_sem.at[0])
    own_b = pltpu.make_async_copy(integ, b_own, local_sem.at[1])
    own_bare = pltpu.make_async_copy(bare_hbm, bare, local_sem.at[2])
    own_a.start()
    own_b.start()
    own_bare.start()

    pl.semaphore_wait(barrier, len(greeted))

    def remote(src, dst, send, recv, who):
        return pltpu.make_async_remote_copy(
            src_ref=src, dst_ref=dst, send_sem=send, recv_sem=recv, device_id=who, device_id_type=MESH)

    def piece(q):
        return pl.ds(pl.multiple_of(q * 32, 32), 32)

    def columns(q):
        return pl.ds(pl.multiple_of(q * depth, depth), depth)

    def b_copy(h, d):
        return remote(
            integ.at[:, pl.ds(h * TILE, TILE)], (b_left, b_right)[d].at[:, pl.ds(h * TILE, TILE)],
            b_send.at[h, d], b_recv.at[h, d], (right, left)[d])

    def f_copy(h, d):
        rows = pl.ds(d * half, half)
        return remote(
            (b_left, b_right)[d].at[rows, pl.ds(h * TILE, TILE)], b_far.at[rows, pl.ds(h * TILE, TILE)],
            f_send.at[h, d], f_recv.at[h, d], (right, left)[d])

    def az_copy(d):
        return remote(
            amp.at[:, columns(mod4(z + d))], a_raw.at[0, 0, piece(z)], az_send.at[d], az_recv.at[z], deep[d])

    def az_arrived(q):
        return remote(
            amp.at[:, columns(q)], a_raw.at[0, 0, piece(q)], az_send.at[0], az_recv.at[q], mate)

    def ay_copy(q, d, first=False):
        src = amp.at[:, columns(z)] if first else a_raw.at[0, 0, piece(q)]
        return remote(
            src, a_raw.at[(3, 1)[d], 0, piece(q)], ay_send.at[d, q], ay_recv.at[d, q], (up, down)[d])

    def am_copy(q, first=False):
        src = amp.at[:, columns(z)] if first else a_raw.at[0, 0, piece(q)]
        return remote(src, a_raw.at[0, 1, piece(q)], am_send.at[q], am_recv.at[q], mate)

    def af_copy(q, d):
        dy = (3, 1)[d]
        return remote(
            a_raw.at[dy, 0, piece(q)], a_raw.at[2, 0, piece(q)], af_send.at[q], af_recv.at[q], (up, down)[d])

    def am_far(q):
        return remote(
            a_raw.at[2, 0, piece(q)], a_raw.at[2, 1, piece(q)], am_send.at[8 + q], am_recv.at[8 + q], mate)

    def am_whole(dy):
        return remote(
            a_raw.at[dy, 0], a_raw.at[dy, 1], am_send.at[3 + dy], am_recv.at[3 + dy], mate)

    def area(s, r):
        start, size = SEGMENTS[s]
        return pl.ds(r * TILE, TILE), pl.ds(start, size)

    def p_copy(s, dy, d):
        rows, where = area(s, d)
        return remote(
            part.at[dy, rows, where], passing.at[d, :, where], p_send.at[s, d], p_recv.at[s, d], (deep[1], deep[3])[d])

    def n_copy(s, dy, d, r):
        rows, where = area(s, r)
        return remote(
            part.at[dy, rows, where], other.at[d, rows, where], n_send.at[s, d, r], n_recv.at[s, d, r],
            (deep[1], deep[3])[d])

    def row_of(s):
        return mod4(z + 8 - y - s)

    column_of = row_of

    def t_copy(s, r, last):
        rows, where = area(s, r)
        return remote(
            total.at[rows, where], (final if last else hop).at[r, :, where], t_send.at[s, r],
            (t_recv if last else h_recv).at[s, r], device(row_of(s), x, lax.rem(c + r, 2), z))

    def h_copy(s, r, straight=False):
        rows, where = area(s, r)
        return remote(
            total.at[rows, where] if straight else hop.at[r, :, where], final.at[r, :, where], h_send.at[s, r],
            t_recv.at[s, r], device(y, x, c, column_of(s)))

    def t_local(s):
        rows, where = area(s, 0)
        return pltpu.make_async_copy(total.at[rows, where], final.at[0, :, where], t_recv.at[s, 0])

    def relay(s):
        @pl.when(mod4(y + s) != 0)
        def _():
            t_copy(s, 1, False).wait_recv()
            h_copy(s, 1).start()

            @pl.when(column_of(s) != y)
            def _():
                t_copy(s, 0, False).wait_recv()
                h_copy(s, 0).start()

    def spot(s, r):
        start, size = SEGMENTS[s]
        return pl.ds(r * TILE, TILE), pl.ds(start, size), pl.ds(start - DIRECT_START, size)

    def y_copy(s, dy, r, final_stop):
        rows, where, there = spot(s, r)
        return remote(
            part.at[dy, rows, where],
            gathered.at[z, rows, there] if final_stop else middle.at[dy, rows, there],
            d_send.at[s, dy, r], d_recv.at[s, z, r] if final_stop else m_recv.at[s, dy, r],
            device(mod4(y + dy), x, lax.rem(c + r, 2), z))

    def z_copy(s, r):
        rows, where, there = spot(s, r)
        return remote(
            part.at[0, rows, where], gathered.at[z, rows, there], d_send.at[s, 0, r], d_recv.at[s, z, r],
            device(y, x, lax.rem(c + r, 2), y))

    def pass_on_product(s, dy, r):
        rows, where, there = spot(s, r)
        return remote(
            middle.at[dy, rows, there], gathered.at[z, rows, there], m_send.at[s, dy, r], d_recv.at[s, z, r],
            device(y, x, c, mod4(y + 4 - dy)))

    def m_arrived(s, dy, r):
        rows, where, there = spot(s, r)
        return remote(
            part.at[0, rows, where], middle.at[dy, rows, there], m_send.at[s, dy, r], m_recv.at[s, dy, r], mate)

    def d_local(s):
        rows, where, there = spot(s, 0)
        return pltpu.make_async_copy(part.at[0, rows, where], gathered.at[z, rows, there], d_recv.at[s, z, 0])

    def d_arrived(s, q, r):
        rows, where, there = spot(s, r)
        return remote(
            part.at[0, rows, where], gathered.at[q, rows, there], d_send.at[s, 0, r], d_recv.at[s, q, r], mate)

    def forward(s):
        for dy in (1, 3, 2):
            @pl.when(mod4(y + 4 - dy) != z)
            def _():
                for r in range(2):
                    m_arrived(s, dy, r).wait_recv()
                    pass_on_product(s, dy, r).start()

    def block_for(s, delta):
        return mod4(z + delta + 16 - 2 * y - s)

    for h in range(2):
        for d in range(2):
            b_copy(h, d).start()
    for d in (1, 3, 2):
        az_copy(d).start()
    for d in range(2):
        ay_copy(z, d, True).start()
    am_copy(z, True).start()

    def split(value):
        hi = value.astype(BF16)
        return hi, (value - hi.astype(F32)).astype(BF16)

    def convert_b(slot, sources):
        @pl.loop(0, depth // 256)
        def _(i):
            rows = pl.ds(pl.multiple_of(i * 256, 256), 256)
            for at, source, start in sources:
                hi, lo = split(source[rows, start:start + TILE])
                b_hi[slot, rows, at:at + TILE] = hi
                b_lo[slot, rows, at:at + TILE] = lo

    def convert_a(dy, rel):
        tile = mod4(y + dy) * 8 + x * 2 + lax.rem(c + rel, 2)
        block = order[tile]

        @pl.loop(0, depth // TILE)
        def _(k):
            keep = pattern[block, z * (depth // TILE) + k].astype(F32)
            where = pl.ds(pl.multiple_of(k * TILE, TILE), TILE)
            hi, lo = split(a_raw[dy, rel, :, where] * keep)
            a_hi[dy, rel * TILE:(rel + 1) * TILE, where] = hi
            a_lo[dy, rel * TILE:(rel + 1) * TILE, where] = lo

    def dot(a, b):
        return jnp.dot(a, b, preferred_element_type=F32)

    def multiply(s, dy):
        start, size = SEGMENTS[s]
        slot, at = start // 256, start % 256
        hi, lo = b_hi[slot, :, at:at + size], b_lo[slot, :, at:at + size]
        left_hi, left_lo = a_hi[dy], a_lo[dy]
        part[dy, :, start:start + size] = dot(left_hi, hi) + (dot(left_hi, lo) + dot(left_lo, hi))

        if s in DIRECT:
            @pl.when(dy == 0)
            def _():
                z_copy(s, 1).start()

                @pl.when(y != z)
                def _():
                    z_copy(s, 0).start()

                @pl.when(y == z)
                def _():
                    d_local(s).start()

            @pl.when(jnp.logical_and(dy != 0, y != z))
            def _():
                for r in range(2):
                    y_copy(s, dy, r, False).start()

            @pl.when(jnp.logical_and(dy != 0, y == z))
            def _():
                for r in range(2):
                    y_copy(s, dy, r, True).start()
        else:
            delta = mod4(2 * y + dy + s + 4 - z)

            @pl.when(delta == 2)
            def _():
                for d in range(2):
                    p_copy(s, dy, d).start()

            @pl.when(delta == 1)
            def _():
                n_copy(s, dy, 0, 1).start()

            @pl.when(delta == 3)
            def _():
                n_copy(s, dy, 1, 0).start()

    def pass_on(s, dy):
        if s in DIRECT:
            return
        start, size = SEGMENTS[s]
        delta = mod4(2 * y + dy + s + 4 - z)
        for d in range(2):
            @pl.when(delta == (1, 3)[d])
            def _():
                p_copy(s, 0, d).wait_recv()
                rows = slice(d * TILE, (d + 1) * TILE)
                part[dy, rows, start:start + size] += passing[d, :, start:start + size]
                n_copy(s, dy, d, d).start()

    def add_up(s):
        start, size = SEGMENTS[s]
        mine = block_for(s, 0)
        for r in (1, 0):
            for d in range(2):
                n_copy(s, 0, d, r).wait_recv()
            rows = slice(r * TILE, (r + 1) * TILE)
            where = slice(start, start + size)
            total[rows, where] = part[mine, rows, where] + (other[0, rows, where] + other[1, rows, where])
            send_total(s, r)

    def send_total(s, r):
        def go(last):
            if r == 1:
                t_copy(s, r, last).start()
            else:
                @pl.when(row_of(s) != y)
                def _():
                    t_copy(s, r, last).start()

                @pl.when(row_of(s) == y)
                def _():
                    if last:
                        t_local(s).start()
                    else:
                        h_copy(s, 0, True).start()

        @pl.when(mod4(row_of(s) + s) == 0)
        def _():
            go(True)

        @pl.when(mod4(row_of(s) + s) != 0)
        def _():
            go(False)

    def finish(s):
        start, size = SEGMENTS[s]
        if s in DIRECT:
            for q in range(4):
                d_arrived(s, q, 1).wait_recv()

                @pl.when(jnp.logical_or(y != z, q != z))
                def _():
                    d_arrived(s, q, 0).wait_recv()

            @pl.when(y == z)
            def _():
                d_local(s).wait()
        else:
            here = jnp.logical_and(mod4(y + s) == 0, y == z)

            @pl.when(jnp.logical_not(here))
            def _():
                h_copy(s, 0).wait_recv()

            @pl.when(here)
            def _():
                t_local(s).wait()

            h_copy(s, 1).wait_recv()
        beside = mod4(x + 3), mod4(x + 1)
        pieces = (
            ((x, 0), (x, 1)), ((beside[0], 0), (beside[1], 0)), ((beside[0], 1), (beside[1], 1)),
            ((mod4(x + 2), 0),), ((mod4(x + 2), 1),))[s]
        for r in range(2):
            for i, (xx, h) in enumerate(pieces):
                place = pl.multiple_of(xx * 512 + lax.rem(c + r, 2) * 256 + h * TILE, TILE)
                where = pl.ds(place, TILE)
                at = start + i * TILE
                if s in DIRECT:
                    at = at - DIRECT_START
                    mine = [gathered[q, r * TILE:(r + 1) * TILE, at:at + TILE] for q in range(4)]
                    value = bare[:, where] + ((mine[0] + mine[1]) + (mine[2] + mine[3]))
                else:
                    value = bare[:, where] + final[r, :, at:at + TILE]
                out[:, where] = -value / (occ_wide[...] + virt[:, where])

    def sent(s):
        if s in DIRECT:
            @pl.when(y != z)
            def _():
                z_copy(s, 0).wait_send()

            z_copy(s, 1).wait_send()

            @pl.loop(1, 4)
            def _(dy):
                for r in range(2):
                    y_copy(s, dy, r, False).wait_send()

                @pl.when(mod4(y + 4 - dy) != z)
                def _():
                    for r in range(2):
                        pass_on_product(s, dy, r).wait_send()
        else:
            for d in range(2):
                p_copy(s, 0, d).wait_send()
                for r in range(2):
                    n_copy(s, 0, d, r).wait_send()
            t_copy(s, 1, True).wait_send()

            @pl.when(row_of(s) != y)
            def _():
                t_copy(s, 0, True).wait_send()

            @pl.when(mod4(y + s) != 0)
            def _():
                for r in range(2):
                    h_copy(s, r).wait_send()

    own_b.wait()
    convert_b(0, ((0, b_own, 0), (TILE, b_own, TILE)))
    occ_wide[...] = jnp.broadcast_to(occ[...], (TILE, TILE)).T
    own_a.wait()

    for d in (1, 3, 2):
        q = mod4(z + d)
        az_arrived(q).wait_recv()
        for to in range(2):
            ay_copy(q, to).start()
        am_copy(q).start()
    convert_a(0, 0)
    for d in (0, 1, 3, 2):
        am_copy(mod4(z + d)).wait_recv()
    convert_a(0, 1)
    multiply(0, jnp.int32(0))

    for q, d in ((z, 0), (mod4(z + 1), 0), (mod4(z + 3), 1), (mod4(z + 2), 1)):
        ay_copy(q, d).wait_recv()
        af_copy(q, d).start()
    for q, d in ((z, 1), (mod4(z + 1), 1), (mod4(z + 3), 0), (mod4(z + 2), 0)):
        ay_copy(q, d).wait_recv()
    am_whole(3).start()
    am_whole(1).start()
    for d in range(2):
        b_copy(0, d).wait_recv()
        f_copy(0, d).start()
    convert_a(3, 0)
    convert_a(1, 0)
    am_whole(3).wait_recv()
    convert_a(3, 1)
    am_whole(1).wait_recv()
    convert_a(1, 1)
    multiply(0, jnp.int32(3))
    multiply(0, jnp.int32(1))
    pass_on(0, 0)
    for q in (z, mod4(z + 3)):
        af_copy(q, 0).wait_recv()
        am_far(q).start()
    convert_b(1, ((0, b_left, 0), (TILE, b_right, 0)))
    for dy in (0, 3, 1):
        multiply(1, jnp.int32(dy))
    for q in (mod4(z + 1), mod4(z + 2)):
        af_copy(q, 0).wait_recv()
        am_far(q).start()
    pass_on(0, 3)
    pass_on(0, 1)
    convert_a(2, 0)
    for d in (0, 1, 3, 2):
        am_far(mod4(z + d)).wait_recv()
    convert_a(2, 1)
    multiply(0, jnp.int32(2))
    multiply(1, jnp.int32(2))
    pass_on(1, 0)
    pass_on(1, 3)
    pass_on(1, 1)

    for d in range(2):
        b_copy(1, d).wait_recv()
        f_copy(1, d).start()
    pass_on(0, 2)
    convert_b(2, ((0, b_left, TILE), (TILE, b_right, TILE)))
    pass_on(1, 2)

    def every(order, action, s):
        @pl.loop(0, 4)
        def _(i):
            action(s, mod4(3 * i + order))

    every(0, multiply, 2)
    every(0, pass_on, 2)
    add_up(0)
    add_up(1)
    own_bare.wait()

    for d in range(2):
        f_copy(0, d).wait_recv()
    convert_b(3, ((0, b_far, 0),))
    every(1, multiply, 3)
    every(1, pass_on, 3)
    add_up(2)
    relay(0)
    relay(1)

    for h in range(2):
        for d in range(2):
            b_copy(h, d).wait_send()
            if h == 0:
                f_copy(h, d).wait_send()
    for d in (1, 2, 3):
        az_copy(d).wait_send()
    for d in (1, 3):
        am_whole(d).wait_send()
    for d in range(4):
        q = mod4(z + d)
        for to in range(2):
            ay_copy(q, to).wait_send()
        am_copy(q).wait_send()
        af_copy(q, 0).wait_send()
        am_far(q).wait_send()
    for d in range(2):
        f_copy(1, d).wait_recv()
    convert_b(3, ((TILE, b_far, TILE),))
    every(2, multiply, 4)
    add_up(3)
    relay(2)
    finish(0)
    forward(4)
    finish(1)
    sent(0)
    sent(1)
    relay(3)
    finish(2)
    finish(3)
    finish(4)

    for d in range(2):
        f_copy(1, d).wait_send()
    for s in range(2, len(SEGMENTS)):
        sent(s)


def shards(amplitudes, integrals, bare_terms, pattern, block_order, occ_gap, virt_gap):
    depth, width = integrals.shape
    rows, columns = bare_terms.shape
    anywhere = pl.BlockSpec(memory_space=pl.ANY)
    vector = pl.BlockSpec(memory_space=pltpu.VMEM)
    scalar = pl.BlockSpec(memory_space=pltpu.SMEM)
    sems = [(3,), (2, 2), (2, 2), (2, 2), (2, 2), (4,), (4,), (2, 4), (2, 4), (4,), (4,), (12,), (12,),
            (5, 2), (5, 2), (5, 2, 2), (5, 2, 2), (5, 2), (5, 2), (5, 2), (5, 2),
            (5, 4, 2), (5, 4, 2), (5, 4, 2), (5, 4, 2)]
    return pl.pallas_call(
        kernel,
        out_shape=jax.ShapeDtypeStruct((rows, columns), F32),
        in_specs=[anywhere, anywhere, anywhere, scalar, scalar, vector, vector],
        out_specs=vector,
        scratch_shapes=[
            pltpu.VMEM((4, 2, TILE, depth), F32),
            pltpu.VMEM((4, 2 * TILE, depth), BF16),
            pltpu.VMEM((4, 2 * TILE, depth), BF16),
            pltpu.VMEM((depth, width), F32),
            pltpu.VMEM((depth, width), F32),
            pltpu.VMEM((depth, width), F32),
            pltpu.VMEM((depth, width), F32),
            pltpu.VMEM((4, depth, width), BF16),
            pltpu.VMEM((4, depth, width), BF16),
            pltpu.VMEM((4, 2 * TILE, 4 * width), F32),
            pltpu.VMEM((2, TILE, 4 * width), F32),
            pltpu.VMEM((2, 2 * TILE, 4 * width), F32),
            pltpu.VMEM((2 * TILE, 4 * width), F32),
            pltpu.VMEM((2, TILE, 4 * width), F32),
            pltpu.VMEM((2, TILE, 4 * width), F32),
            pltpu.VMEM((4, 2 * TILE, width), F32),
            pltpu.VMEM((4, 2 * TILE, width), F32),
            pltpu.VMEM((rows, columns), F32),
            pltpu.VMEM((TILE, TILE), F32),
        ] + [pltpu.SemaphoreType.DMA(shape) for shape in sems],
        compiler_params=pltpu.CompilerParams(
            collective_id=0, has_side_effects=True, vmem_limit_bytes=58 * 2**20),
        name="ladder",
    )(amplitudes, integrals, bare_terms, pattern, block_order, occ_gap.reshape(1, -1), virt_gap.reshape(1, -1))


def solution(mesh):
    placed = (
        P(("wide", "narrow"), None),
        P("narrow", "wide"),
        P("wide", "narrow"),
        P(),
        P(),
        P("wide"),
        P("narrow"),
    )
    return jax.shard_map(
        shards, mesh=mesh, in_specs=placed, out_specs=P("wide", "narrow"), check_vma=False
    )
```

```python
import jax
import jax.numpy as jnp
from jax import lax
from jax.experimental import pallas as pl
from jax.experimental.pallas import tpu as pltpu
from jax.sharding import PartitionSpec as P

TILE = 128
MESH = pl.DeviceIdType.MESH
SEGMENTS = ((0, 256), (256, 256), (512, 256), (768, 128), (896, 128))
DIRECT = (4,)
DIRECT_START = 768
F32 = jnp.float32
BF16 = jnp.bfloat16


def kernel(
    amp, integ, bare_hbm, pattern, order, occ, virt, out,
    a_raw, a_hi, a_lo, b_own, b_left, b_right, b_far, b_hi, b_lo, part, passing, other, total, hop, final, middle, gathered, bare, occ_wide,
    local_sem, b_send, b_recv, f_send, f_recv, az_send, az_recv, ay_send, ay_recv, af_send, af_recv,
    am_send, am_recv, p_send, p_recv, n_send, n_recv, t_send, t_recv, h_send, h_recv,
    d_send, d_recv, m_send, m_recv,
):
    w = lax.axis_index("wide")
    z = lax.axis_index("narrow")
    y = lax.div(w, 8)
    x = lax.rem(lax.div(w, 2), 4)
    c = lax.rem(w, 2)
    depth = integ.shape[0]
    half = depth // 2

    def device(yy, xx, cc, zz):
        return (yy * 8 + xx * 2 + cc, zz)

    def mod4(v):
        return lax.rem(v, 4)

    right, left = device(y, mod4(x + 1), c, z), device(y, mod4(x + 3), c, z)
    up, down = device(mod4(y + 1), x, c, z), device(mod4(y + 3), x, c, z)
    mate = device(y, x, 1 - c, z)
    deep = [None] + [device(y, x, c, mod4(z + d)) for d in (1, 2, 3)]
    barrier = pltpu.get_barrier_semaphore()
    greeted = [right, left, mate]
    for d in (1, 2, 3):
        for cc in (c, 1 - c):
            greeted += [device(mod4(y + d), x, cc, z), device(y, x, cc, mod4(z + d))]
    for who in greeted:
        pl.semaphore_signal(barrier, inc=1, device_id=who, device_id_type=MESH)

    own_a = pltpu.make_async_copy(
        amp.at[:, pl.ds(pl.multiple_of(z * depth, depth), depth)],
        a_raw.at[0, 0, pl.ds(pl.multiple_of(z * 32, 32), 32)], local_sem.at[0])
    own_b = pltpu.make_async_copy(integ, b_own, local_sem.at[1])
    own_bare = pltpu.make_async_copy(bare_hbm, bare, local_sem.at[2])
    own_a.start()
    own_b.start()
    own_bare.start()

    pl.semaphore_wait(barrier, len(greeted))

    def remote(src, dst, send, recv, who):
        return pltpu.make_async_remote_copy(
            src_ref=src, dst_ref=dst, send_sem=send, recv_sem=recv, device_id=who, device_id_type=MESH)

    def piece(q):
        return pl.ds(pl.multiple_of(q * 32, 32), 32)

    def columns(q):
        return pl.ds(pl.multiple_of(q * depth, depth), depth)

    def b_copy(h, d):
        return remote(
            integ.at[:, pl.ds(h * TILE, TILE)], (b_left, b_right)[d].at[:, pl.ds(h * TILE, TILE)],
            b_send.at[h, d], b_recv.at[h, d], (right, left)[d])

    def f_copy(h, d):
        rows = pl.ds(d * half, half)
        return remote(
            (b_left, b_right)[d].at[rows, pl.ds(h * TILE, TILE)], b_far.at[rows, pl.ds(h * TILE, TILE)],
            f_send.at[h, d], f_recv.at[h, d], (right, left)[d])

    def az_copy(d):
        return remote(
            amp.at[:, columns(mod4(z + d))], a_raw.at[0, 0, piece(z)], az_send.at[d], az_recv.at[z], deep[d])

    def az_arrived(q):
        return remote(
            amp.at[:, columns(q)], a_raw.at[0, 0, piece(q)], az_send.at[0], az_recv.at[q], mate)

    def ay_copy(q, d, first=False):
        src = amp.at[:, columns(z)] if first else a_raw.at[0, 0, piece(q)]
        return remote(
            src, a_raw.at[(3, 1)[d], 0, piece(q)], ay_send.at[d, q], ay_recv.at[d, q], (up, down)[d])

    def am_copy(q, first=False):
        src = amp.at[:, columns(z)] if first else a_raw.at[0, 0, piece(q)]
        return remote(src, a_raw.at[0, 1, piece(q)], am_send.at[q], am_recv.at[q], mate)

    def af_copy(q, d):
        dy = (3, 1)[d]
        return remote(
            a_raw.at[dy, 0, piece(q)], a_raw.at[2, 0, piece(q)], af_send.at[q], af_recv.at[q], (up, down)[d])

    def am_far(q):
        return remote(
            a_raw.at[2, 0, piece(q)], a_raw.at[2, 1, piece(q)], am_send.at[8 + q], am_recv.at[8 + q], mate)

    def am_whole(dy):
        return remote(
            a_raw.at[dy, 0], a_raw.at[dy, 1], am_send.at[3 + dy], am_recv.at[3 + dy], mate)

    def area(s, r):
        start, size = SEGMENTS[s]
        return pl.ds(r * TILE, TILE), pl.ds(start, size)

    def p_copy(s, dy, d):
        rows, where = area(s, d)
        return remote(
            part.at[dy, rows, where], passing.at[d, :, where], p_send.at[s, d], p_recv.at[s, d], (deep[1], deep[3])[d])

    def n_copy(s, dy, d, r):
        rows, where = area(s, r)
        return remote(
            part.at[dy, rows, where], other.at[d, rows, where], n_send.at[s, d, r], n_recv.at[s, d, r],
            (deep[1], deep[3])[d])

    def row_of(s):
        return mod4(z + 8 - y - s)

    column_of = row_of

    def t_copy(s, r, last):
        rows, where = area(s, r)
        return remote(
            total.at[rows, where], (final if last else hop).at[r, :, where], t_send.at[s, r],
            (t_recv if last else h_recv).at[s, r], device(row_of(s), x, lax.rem(c + r, 2), z))

    def h_copy(s, r, straight=False):
        rows, where = area(s, r)
        return remote(
            total.at[rows, where] if straight else hop.at[r, :, where], final.at[r, :, where], h_send.at[s, r],
            t_recv.at[s, r], device(y, x, c, column_of(s)))

    def t_local(s):
        rows, where = area(s, 0)
        return pltpu.make_async_copy(total.at[rows, where], final.at[0, :, where], t_recv.at[s, 0])

    def relay(s):
        @pl.when(mod4(y + s) != 0)
        def _():
            t_copy(s, 1, False).wait_recv()
            h_copy(s, 1).start()

            @pl.when(column_of(s) != y)
            def _():
                t_copy(s, 0, False).wait_recv()
                h_copy(s, 0).start()

    def spot(s, r):
        start, size = SEGMENTS[s]
        return pl.ds(r * TILE, TILE), pl.ds(start, size), pl.ds(start - DIRECT_START, size)

    def y_copy(s, dy, r, final_stop):
        rows, where, there = spot(s, r)
        return remote(
            part.at[dy, rows, where],
            gathered.at[z, rows, there] if final_stop else middle.at[dy, rows, there],
            d_send.at[s, dy, r], d_recv.at[s, z, r] if final_stop else m_recv.at[s, dy, r],
            device(mod4(y + dy), x, lax.rem(c + r, 2), z))

    def z_copy(s, r):
        rows, where, there = spot(s, r)
        return remote(
            part.at[0, rows, where], gathered.at[z, rows, there], d_send.at[s, 0, r], d_recv.at[s, z, r],
            device(y, x, lax.rem(c + r, 2), y))

    def pass_on_product(s, dy, r):
        rows, where, there = spot(s, r)
        return remote(
            middle.at[dy, rows, there], gathered.at[z, rows, there], m_send.at[s, dy, r], d_recv.at[s, z, r],
            device(y, x, c, mod4(y + 4 - dy)))

    def m_arrived(s, dy, r):
        rows, where, there = spot(s, r)
        return remote(
            part.at[0, rows, where], middle.at[dy, rows, there], m_send.at[s, dy, r], m_recv.at[s, dy, r], mate)

    def d_local(s):
        rows, where, there = spot(s, 0)
        return pltpu.make_async_copy(part.at[0, rows, where], gathered.at[z, rows, there], d_recv.at[s, z, 0])

    def d_arrived(s, q, r):
        rows, where, there = spot(s, r)
        return remote(
            part.at[0, rows, where], gathered.at[q, rows, there], d_send.at[s, 0, r], d_recv.at[s, q, r], mate)

    def forward(s):
        for dy in (1, 3, 2):
            @pl.when(mod4(y + 4 - dy) != z)
            def _():
                for r in range(2):
                    m_arrived(s, dy, r).wait_recv()
                    pass_on_product(s, dy, r).start()

    def block_for(s, delta):
        return mod4(z + delta + 16 - 2 * y - s)

    for h in range(2):
        for d in range(2):
            b_copy(h, d).start()
    for d in (1, 3, 2):
        az_copy(d).start()
    for d in range(2):
        ay_copy(z, d, True).start()
    am_copy(z, True).start()

    def split(value):
        hi = value.astype(BF16)
        return hi, (value - hi.astype(F32)).astype(BF16)

    def convert_b(slot, sources):
        @pl.loop(0, depth // 256)
        def _(i):
            rows = pl.ds(pl.multiple_of(i * 256, 256), 256)
            for at, source, start in sources:
                hi, lo = split(source[rows, start:start + TILE])
                b_hi[slot, rows, at:at + TILE] = hi
                b_lo[slot, rows, at:at + TILE] = lo

    def convert_a(dy, rel):
        tile = mod4(y + dy) * 8 + x * 2 + lax.rem(c + rel, 2)
        block = order[tile]

        @pl.loop(0, depth // TILE)
        def _(k):
            keep = pattern[block, z * (depth // TILE) + k].astype(F32)
            where = pl.ds(pl.multiple_of(k * TILE, TILE), TILE)
            hi, lo = split(a_raw[dy, rel, :, where] * keep)
            a_hi[dy, rel * TILE:(rel + 1) * TILE, where] = hi
            a_lo[dy, rel * TILE:(rel + 1) * TILE, where] = lo

    def dot(a, b):
        return jnp.dot(a, b, preferred_element_type=F32)

    def multiply(s, dy):
        start, size = SEGMENTS[s]
        slot, at = start // 256, start % 256
        hi, lo = b_hi[slot, :, at:at + size], b_lo[slot, :, at:at + size]
        left_hi, left_lo = a_hi[dy], a_lo[dy]
        part[dy, :, start:start + size] = dot(left_hi, hi) + (dot(left_hi, lo) + dot(left_lo, hi))

        if s in DIRECT:
            @pl.when(dy == 0)
            def _():
                z_copy(s, 1).start()

                @pl.when(y != z)
                def _():
                    z_copy(s, 0).start()

                @pl.when(y == z)
                def _():
                    d_local(s).start()

            @pl.when(jnp.logical_and(dy != 0, y != z))
            def _():
                for r in range(2):
                    y_copy(s, dy, r, False).start()

            @pl.when(jnp.logical_and(dy != 0, y == z))
            def _():
                for r in range(2):
                    y_copy(s, dy, r, True).start()
        else:
            delta = mod4(2 * y + dy + s + 4 - z)

            @pl.when(delta == 2)
            def _():
                for d in range(2):
                    p_copy(s, dy, d).start()

            @pl.when(delta == 1)
            def _():
                n_copy(s, dy, 0, 1).start()

            @pl.when(delta == 3)
            def _():
                n_copy(s, dy, 1, 0).start()

    def pass_on(s, dy):
        if s in DIRECT:
            return
        start, size = SEGMENTS[s]
        delta = mod4(2 * y + dy + s + 4 - z)
        for d in range(2):
            @pl.when(delta == (1, 3)[d])
            def _():
                p_copy(s, 0, d).wait_recv()
                rows = slice(d * TILE, (d + 1) * TILE)
                part[dy, rows, start:start + size] += passing[d, :, start:start + size]
                n_copy(s, dy, d, d).start()

    def add_up(s):
        start, size = SEGMENTS[s]
        mine = block_for(s, 0)
        for r in (1, 0):
            for d in range(2):
                n_copy(s, 0, d, r).wait_recv()
            rows = slice(r * TILE, (r + 1) * TILE)
            where = slice(start, start + size)
            total[rows, where] = part[mine, rows, where] + (other[0, rows, where] + other[1, rows, where])
            send_total(s, r)

    def send_total(s, r):
        def go(last):
            if r == 1:
                t_copy(s, r, last).start()
            else:
                @pl.when(row_of(s) != y)
                def _():
                    t_copy(s, r, last).start()

                @pl.when(row_of(s) == y)
                def _():
                    if last:
                        t_local(s).start()
                    else:
                        h_copy(s, 0, True).start()

        @pl.when(mod4(row_of(s) + s) == 0)
        def _():
            go(True)

        @pl.when(mod4(row_of(s) + s) != 0)
        def _():
            go(False)

    def finish(s):
        start, size = SEGMENTS[s]
        if s in DIRECT:
            for q in range(4):
                d_arrived(s, q, 1).wait_recv()

                @pl.when(jnp.logical_or(y != z, q != z))
                def _():
                    d_arrived(s, q, 0).wait_recv()

            @pl.when(y == z)
            def _():
                d_local(s).wait()
        else:
            here = jnp.logical_and(mod4(y + s) == 0, y == z)

            @pl.when(jnp.logical_not(here))
            def _():
                h_copy(s, 0).wait_recv()

            @pl.when(here)
            def _():
                t_local(s).wait()

            h_copy(s, 1).wait_recv()
        beside = mod4(x + 3), mod4(x + 1)
        pieces = (
            ((x, 0), (x, 1)), ((beside[0], 0), (beside[1], 0)), ((beside[0], 1), (beside[1], 1)),
            ((mod4(x + 2), 0),), ((mod4(x + 2), 1),))[s]
        for r in range(2):
            for i, (xx, h) in enumerate(pieces):
                place = pl.multiple_of(xx * 512 + lax.rem(c + r, 2) * 256 + h * TILE, TILE)
                where = pl.ds(place, TILE)
                at = start + i * TILE
                if s in DIRECT:
                    at = at - DIRECT_START
                    mine = [gathered[q, r * TILE:(r + 1) * TILE, at:at + TILE] for q in range(4)]
                    value = bare[:, where] + ((mine[0] + mine[1]) + (mine[2] + mine[3]))
                else:
                    value = bare[:, where] + final[r, :, at:at + TILE]
                out[:, where] = -value / (occ_wide[...] + virt[:, where])

    def sent(s):
        if s in DIRECT:
            @pl.when(y != z)
            def _():
                z_copy(s, 0).wait_send()

            z_copy(s, 1).wait_send()

            @pl.loop(1, 4)
            def _(dy):
                for r in range(2):
                    y_copy(s, dy, r, False).wait_send()

                @pl.when(mod4(y + 4 - dy) != z)
                def _():
                    for r in range(2):
                        pass_on_product(s, dy, r).wait_send()
        else:
            for d in range(2):
                p_copy(s, 0, d).wait_send()
                for r in range(2):
                    n_copy(s, 0, d, r).wait_send()
            t_copy(s, 1, True).wait_send()

            @pl.when(row_of(s) != y)
            def _():
                t_copy(s, 0, True).wait_send()

            @pl.when(mod4(y + s) != 0)
            def _():
                for r in range(2):
                    h_copy(s, r).wait_send()

    own_b.wait()
    convert_b(0, ((0, b_own, 0), (TILE, b_own, TILE)))
    occ_wide[...] = jnp.broadcast_to(occ[...], (TILE, TILE)).T
    own_a.wait()

    for d in (1, 3, 2):
        q = mod4(z + d)
        az_arrived(q).wait_recv()
        for to in range(2):
            ay_copy(q, to).start()
        am_copy(q).start()
    convert_a(0, 0)
    for d in (0, 1, 3, 2):
        am_copy(mod4(z + d)).wait_recv()
    convert_a(0, 1)
    multiply(0, jnp.int32(0))

    for q, d in ((z, 0), (mod4(z + 1), 0), (mod4(z + 3), 1), (mod4(z + 2), 1)):
        ay_copy(q, d).wait_recv()
        af_copy(q, d).start()
    for q, d in ((z, 1), (mod4(z + 1), 1), (mod4(z + 3), 0), (mod4(z + 2), 0)):
        ay_copy(q, d).wait_recv()
    am_whole(3).start()
    am_whole(1).start()
    for d in range(2):
        b_copy(0, d).wait_recv()
        f_copy(0, d).start()
    convert_a(3, 0)
    convert_a(1, 0)
    am_whole(3).wait_recv()
    convert_a(3, 1)
    am_whole(1).wait_recv()
    convert_a(1, 1)
    multiply(0, jnp.int32(3))
    multiply(0, jnp.int32(1))
    pass_on(0, 0)
    for q in (z, mod4(z + 3)):
        af_copy(q, 0).wait_recv()
        am_far(q).start()
    convert_b(1, ((0, b_left, 0), (TILE, b_right, 0)))
    for dy in (0, 3, 1):
        multiply(1, jnp.int32(dy))
    for q in (mod4(z + 1), mod4(z + 2)):
        af_copy(q, 0).wait_recv()
        am_far(q).start()
    pass_on(0, 3)
    pass_on(0, 1)
    convert_a(2, 0)
    for d in (0, 1, 3, 2):
        am_far(mod4(z + d)).wait_recv()
    convert_a(2, 1)
    multiply(0, jnp.int32(2))
    multiply(1, jnp.int32(2))
    pass_on(1, 0)
    pass_on(1, 3)
    pass_on(1, 1)

    for d in range(2):
        b_copy(1, d).wait_recv()
        f_copy(1, d).start()
    pass_on(0, 2)
    convert_b(2, ((0, b_left, TILE), (TILE, b_right, TILE)))
    pass_on(1, 2)

    def every(order, action, s):
        @pl.loop(0, 4)
        def _(i):
            action(s, mod4(3 * i + order))

    def far_first(s):
        @pl.loop(0, 4)
        def _(i):
            multiply(s, block_for(s, mod4(2 + 3 * i)))

    far_first(2)
    every(0, pass_on, 2)
    add_up(0)
    add_up(1)
    own_bare.wait()

    for d in range(2):
        f_copy(0, d).wait_recv()
    convert_b(3, ((0, b_far, 0),))
    far_first(3)
    every(1, pass_on, 3)
    add_up(2)
    relay(0)
    relay(1)

    for h in range(2):
        for d in range(2):
            b_copy(h, d).wait_send()
            if h == 0:
                f_copy(h, d).wait_send()
    for d in (1, 2, 3):
        az_copy(d).wait_send()
    for d in (1, 3):
        am_whole(d).wait_send()
    for d in range(4):
        q = mod4(z + d)
        for to in range(2):
            ay_copy(q, to).wait_send()
        am_copy(q).wait_send()
        af_copy(q, 0).wait_send()
        am_far(q).wait_send()
    for d in range(2):
        f_copy(1, d).wait_recv()
    convert_b(3, ((TILE, b_far, TILE),))
    every(2, multiply, 4)
    add_up(3)
    relay(2)
    finish(0)
    forward(4)
    finish(1)
    sent(0)
    sent(1)
    relay(3)
    finish(2)
    finish(3)
    finish(4)

    for d in range(2):
        f_copy(1, d).wait_send()
    for s in range(2, len(SEGMENTS)):
        sent(s)


def shards(amplitudes, integrals, bare_terms, pattern, block_order, occ_gap, virt_gap):
    depth, width = integrals.shape
    rows, columns = bare_terms.shape
    anywhere = pl.BlockSpec(memory_space=pl.ANY)
    vector = pl.BlockSpec(memory_space=pltpu.VMEM)
    scalar = pl.BlockSpec(memory_space=pltpu.SMEM)
    sems = [(3,), (2, 2), (2, 2), (2, 2), (2, 2), (4,), (4,), (2, 4), (2, 4), (4,), (4,), (12,), (12,),
            (5, 2), (5, 2), (5, 2, 2), (5, 2, 2), (5, 2), (5, 2), (5, 2), (5, 2),
            (5, 4, 2), (5, 4, 2), (5, 4, 2), (5, 4, 2)]
    return pl.pallas_call(
        kernel,
        out_shape=jax.ShapeDtypeStruct((rows, columns), F32),
        in_specs=[anywhere, anywhere, anywhere, scalar, scalar, vector, vector],
        out_specs=vector,
        scratch_shapes=[
            pltpu.VMEM((4, 2, TILE, depth), F32),
            pltpu.VMEM((4, 2 * TILE, depth), BF16),
            pltpu.VMEM((4, 2 * TILE, depth), BF16),
            pltpu.VMEM((depth, width), F32),
            pltpu.VMEM((depth, width), F32),
            pltpu.VMEM((depth, width), F32),
            pltpu.VMEM((depth, width), F32),
            pltpu.VMEM((4, depth, width), BF16),
            pltpu.VMEM((4, depth, width), BF16),
            pltpu.VMEM((4, 2 * TILE, 4 * width), F32),
            pltpu.VMEM((2, TILE, 4 * width), F32),
            pltpu.VMEM((2, 2 * TILE, 4 * width), F32),
            pltpu.VMEM((2 * TILE, 4 * width), F32),
            pltpu.VMEM((2, TILE, 4 * width), F32),
            pltpu.VMEM((2, TILE, 4 * width), F32),
            pltpu.VMEM((4, 2 * TILE, width), F32),
            pltpu.VMEM((4, 2 * TILE, width), F32),
            pltpu.VMEM((rows, columns), F32),
            pltpu.VMEM((TILE, TILE), F32),
        ] + [pltpu.SemaphoreType.DMA(shape) for shape in sems],
        compiler_params=pltpu.CompilerParams(
            collective_id=0, has_side_effects=True, vmem_limit_bytes=58 * 2**20),
        name="ladder",
    )(amplitudes, integrals, bare_terms, pattern, block_order, occ_gap.reshape(1, -1), virt_gap.reshape(1, -1))


def solution(mesh):
    placed = (
        P(("wide", "narrow"), None),
        P("narrow", "wide"),
        P("wide", "narrow"),
        P(),
        P(),
        P("wide"),
        P("narrow"),
    )
    return jax.shard_map(
        shards, mesh=mesh, in_specs=placed, out_specs=P("wide", "narrow"), check_vma=False
    )
```
